32 devices in a mesh: seq: 8 (over z, y), head: 4 (over x, core).
Axes of the slice: x: 2, y: 2, z: 4, core: 2. Of those that a mesh axis runs over, the one named last changes fastest.
Arguments:
- queries: bfloat16 [4096, 32, 128], P('seq', 'head'), may hold values from -6 to 6
- key_vectors: bfloat16 [4096, 32, 128], P('seq', 'head'), may hold values from -6 to 6
- value_vectors: bfloat16 [4096, 32, 128], P('seq', 'head'), may hold values from -6 to 6
- doc_ids: int32 [4096], P('seq'), may hold values from 0 to 2, never falling along the last dimension, each value on 1 to 2048 neighbouring positions
- out_weight: bfloat16 [4096, 3072], P('head'), may hold values from -0.09375 to 0.09375
- grad_out: bfloat16 [4096, 3072], P('seq', 'head'), may hold values from -6 to 6
Outputs:
- layer_out: bfloat16 [4096, 3072], P('seq', 'head')
- grad_queries: bfloat16 [4096, 32, 128], P('seq', 'head')
- grad_keys: bfloat16 [4096, 32, 128], P('seq', 'head')
- grad_values: bfloat16 [4096, 32, 128], P('seq', 'head')
- grad_weight: float32 [4096, 3072], P('head', 'seq')
The draws below stay inside these ranges and needn't reach their ends.
Inputs may be any that keep to these rules, and one draw needn't show every extreme that they name: doc_ids never falls; each of the 3 documents has 1 to 2048 tokens and one has exactly 2048.
All inputs are finite; a program needn't handle non-finite values.
Results may differ from the reference program's by a relative error of at most 0.0063.
Values may be sent and summed in bfloat16 or wider, within the bound.
A program may use at most 128 MiB of HBM per device.

```python
import math
import jax
import jax.numpy as jnp
import numpy as np
from jax import lax

DH = 128
HEADS = 32
DM = 3072
TOK_DEV = 512
TOKENS = 4096
HD = 4096
DOCS = 3
DOC_MOST = 2048


def steps_of(key, shape, shards, smallest, high):
    def one(position, blocks):
        heights = jax.random.uniform(jax.random.fold_in(jax.random.fold_in(key, 6), position), (blocks,), jnp.float32, smallest / len(shards), high / len(shards))
        return jnp.repeat(jnp.exp(heights), shape[position] // blocks).reshape((-1,) + (1,) * (len(shape) - position - 1))

    level = one(*shards[0])
    for cut in shards[1:]:
        level = level * one(*cut)
    return level


def length_profile(count, total, bound, slope):
    loads = [(1 << 20) // math.isqrt(grade ** slope) + 1 for grade in range(2, count + 1)]
    rest, counts = total - bound - (count - 1), [1] * (count - 1)
    while rest > 0:
        candidates = [i for i in range(count - 1) if counts[i] < bound]
        pool, left = sum([loads[i] for i in candidates]), rest
        for i in candidates:
            addition = min(bound - counts[i], max(1, left * loads[i] // pool), rest)
            counts[i] = counts[i] + addition
            rest = rest - addition
    return np.array([bound] + counts)


def ragged(stream_key, count, total, bound, lean):
    if count == 2:
        one = jax.random.randint(stream_key, (), max(1, total - bound), min(bound, total - 1) + 1)
        return jnp.stack([one, total - one])
    lengths = jnp.asarray(length_profile(count, total, bound, lean), jnp.int32)
    couples = (count - 1) // 2
    source_of, taker = lengths[1:1 + 2 * couples:2], lengths[2:2 + 2 * couples:2]
    margin = jnp.minimum(source_of - 1, bound - taker)
    shifted = jax.random.randint(jax.random.fold_in(stream_key, 1), (couples,), 0, 1 << 20) % (margin + 1)
    lengths = lengths.at[1:1 + 2 * couples:2].set(source_of - shifted).at[2:2 + 2 * couples:2].set(taker + shifted)
    return lengths[jax.random.permutation(jax.random.fold_in(stream_key, 2), count)]


def scatter_about(own_key, extent, scale, most, shards=(), held_as=jnp.bfloat16):
    entries = scale * jax.random.normal(own_key, extent, jnp.float32)
    if shards:
        entries = entries * steps_of(own_key, extent, shards, -0.22, 0.18)
    return jnp.clip(entries, -most, most).astype(held_as)


def setup_inputs(seed: int = 0) -> dict:
    seeds = jax.random.split(jax.random.key(seed), 7)
    queries = scatter_about(seeds[0], (TOKENS, HEADS, DH), 1.0, 6.0, ((0, 8), (1, 4)))
    key_vectors = scatter_about(seeds[1], (TOKENS, HEADS, DH), 1.0, 6.0, ((0, 8), (1, 4)))
    value_vectors = scatter_about(seeds[2], (TOKENS, HEADS, DH), 1.0, 6.0, ((0, 8), (1, 4)))
    doc_ids = jnp.searchsorted(jnp.cumsum(ragged(seeds[3], DOCS, TOKENS, DOC_MOST, 0)), jnp.arange(TOKENS), side="right").astype(jnp.int32)
    out_weight = scatter_about(seeds[4], (HD, DM), HD ** -0.5, 0.09375, ((0, 4),))
    grad_out = scatter_about(seeds[5], (TOKENS, DM), 1.0, 6.0, ((0, 8), (1, 4)))
    return {"queries": queries, "key_vectors": key_vectors, "value_vectors": value_vectors, "doc_ids": doc_ids, "out_weight": out_weight, "grad_out": grad_out}


def combine(earlier, later):
    same = (earlier[0] == later[0]).astype(jnp.float32)
    return (later[0], later[1] + same[0] * earlier[1])

def reference(queries, key_vectors, value_vectors, doc_ids, out_weight, grad_out):
    blocks = TOKENS // TOK_DEV
    query_blocks = queries.reshape(blocks, TOK_DEV, HEADS, DH)
    key_blocks = key_vectors.reshape(blocks, TOK_DEV, HEADS, DH)
    value_blocks = value_vectors.reshape(blocks, TOK_DEV, HEADS, DH)
    doc_blocks = doc_ids.astype(jnp.float32).reshape(blocks, TOK_DEV)
    causal = lax.broadcasted_iota(jnp.int32, (TOK_DEV, TOK_DEV), 0) >= lax.broadcasted_iota(jnp.int32, (TOK_DEV, TOK_DEV), 1)
    start = (jnp.full((1,), -1.0, jnp.float32), jnp.zeros((HEADS, DH, DH), jnp.float32))

    def scores_of(query_f, key_f, doc_row):
        pairs = causal & (doc_row[:, None] == doc_row[None, :])
        scores = jnp.einsum('thd,shd->hts', query_f, key_f)
        return (jnp.where(pairs[None], scores, 0.0).astype(jnp.bfloat16), pairs)

    def forward_step(carry, inputs):
        query_blk, key_blk, value_blk, doc_row = inputs
        query_f = query_blk.astype(jnp.float32)
        key_f = key_blk.astype(jnp.float32)
        value_f = value_blk.astype(jnp.float32)
        state_low = carry[1].astype(jnp.bfloat16).astype(jnp.float32)
        reads = (doc_row == carry[0][0]).astype(jnp.float32)
        scores_low, pairs = scores_of(query_f, key_f, doc_row)
        attn = jnp.einsum('hts,she->the', scores_low.astype(jnp.float32), value_f)
        attn = attn + reads[:, None, None] * jnp.einsum('thd,hde->the', query_f, state_low)
        tail = (doc_row == doc_row[-1]).astype(jnp.float32)
        own_state = jnp.einsum('shd,she->hde', key_f * tail[:, None, None], value_f)
        return (combine(carry, (doc_row[-1:], own_state)), (attn, carry[1], carry[0]))
    last_carry, (attn, state_in, prev_doc) = lax.scan(forward_step, start, (query_blocks, key_blocks, value_blocks, doc_blocks))
    attn = attn.reshape(TOKENS, HEADS, DH)
    scale = lax.rsqrt(lax.optimization_barrier(jnp.mean(attn * attn, axis=-1, keepdims=True)) + 1e-05)
    normed_f = attn * scale
    normed = normed_f.astype(jnp.bfloat16).reshape(TOKENS, HD)
    layer_out = jnp.dot(normed, out_weight, preferred_element_type=jnp.float32).astype(jnp.bfloat16)
    grad_normed = lax.dot_general(grad_out, out_weight, (((1,), (1,)), ((), ())), preferred_element_type=jnp.float32).reshape(TOKENS, HEADS, DH)
    grad_attn = (scale * (grad_normed - normed_f * lax.optimization_barrier(jnp.mean(grad_normed * normed_f, axis=-1, keepdims=True)))).astype(jnp.bfloat16)
    grad_weight = lax.dot_general(normed, grad_out, (((0,), (0,)), ((), ())), preferred_element_type=jnp.float32)
    grad_blocks = grad_attn.reshape(blocks, TOK_DEV, HEADS, DH)

    def backward_step(carry, inputs):
        query_blk, key_blk, value_blk, doc_row, grad_blk, state_blk, prev_blk = inputs
        query_f = query_blk.astype(jnp.float32)
        key_f = key_blk.astype(jnp.float32)
        value_f = value_blk.astype(jnp.float32)
        grad_f = grad_blk.astype(jnp.float32)
        state_low = state_blk.astype(jnp.bfloat16).astype(jnp.float32)
        back_low = carry[1].astype(jnp.bfloat16).astype(jnp.float32)
        reads = (doc_row == prev_blk[0]).astype(jnp.float32)
        writes = (doc_row == carry[0][0]).astype(jnp.float32)
        scores_low, pairs = scores_of(query_f, key_f, doc_row)
        grad_scores = jnp.einsum('the,she->hts', grad_f, value_f)
        grad_scores = jnp.where(pairs[None], grad_scores, 0.0).astype(jnp.bfloat16).astype(jnp.float32)
        grad_q = jnp.einsum('hts,shd->thd', grad_scores, key_f) + reads[:, None, None] * jnp.einsum('the,hde->thd', grad_f, state_low)
        grad_k = jnp.einsum('hts,thd->shd', grad_scores, query_f) + writes[:, None, None] * jnp.einsum('she,hde->shd', value_f, back_low)
        grad_v = jnp.einsum('hts,the->she', scores_low.astype(jnp.float32), grad_f) + writes[:, None, None] * jnp.einsum('shd,hde->she', key_f, back_low)
        head_mask = (doc_row == doc_row[0]).astype(jnp.float32)
        own_state = jnp.einsum('thd,the->hde', query_f * head_mask[:, None, None], grad_f)
        outs = (grad_q.astype(jnp.bfloat16), grad_k.astype(jnp.bfloat16), grad_v.astype(jnp.bfloat16))
        return (combine(carry, (doc_row[:1], own_state)), outs)
    final_carry, (grad_q, grad_k, grad_v) = lax.scan(backward_step, start, (query_blocks, key_blocks, value_blocks, doc_blocks, grad_blocks, state_in, prev_doc), reverse=True)
    shape = (TOKENS, HEADS, DH)
    return (layer_out, grad_q.reshape(shape), grad_k.reshape(shape), grad_v.reshape(shape), grad_weight)
```

```python
import jax
import jax.numpy as jnp
from jax import lax
from jax.sharding import PartitionSpec as P


BF = jnp.bfloat16
F32 = jnp.float32


def shift(block, distance):
    n = lax.axis_size("seq")
    route = [(i, i + distance) for i in range(n) if 0 <= i + distance < n]
    return lax.ppermute(block, "seq", route)


def swap(block, axis, bit):
    n = lax.axis_size(axis)
    return lax.ppermute(block, axis, [(i, i ^ bit) for i in range(n)])


def gather_heads(block):
    me = lax.axis_index("head")
    bit = lax.axis_size("head") // 2
    tokens, columns = block.shape
    held = block[:, None]
    while bit:
        other = swap(held, "head", bit)
        high = (me // bit) % 2 == 1
        held = jnp.stack([jnp.where(high, other, held), jnp.where(high, held, other)], axis=2)
        held = held.reshape(tokens, -1, columns)
        bit //= 2
    return held


def scatter_heads(partial):
    me = lax.axis_index("head")
    tokens, columns = partial.shape
    size = lax.axis_size("head")
    share = columns // size
    held = partial.reshape(tokens, size, share)
    bit = 1
    while bit < size:
        held = held.reshape(tokens, -1, 2, share)
        mine = (me // bit) % 2
        given = lax.dynamic_index_in_dim(held, 1 - mine, 2, keepdims=False).astype(BF)
        kept = lax.dynamic_index_in_dim(held, mine, 2, keepdims=False)
        held = kept + swap(given, "head", bit).astype(F32)
        bit *= 2
    return held.reshape(tokens, share).astype(BF)


def window(own, doc, sign):
    near = shift(doc, sign)
    total = shift(own.astype(BF), sign)
    span = 1
    while span < lax.axis_size("seq") // 2:
        far_doc = shift(doc, sign * (1 + span))
        far = shift(total, sign * span)
        total = total + jnp.where(far_doc == near, far, jnp.zeros_like(far))
        span *= 2
    return total, near


def shards(queries, key_vectors, value_vectors, doc_ids, out_weight, grad_out):
    n = lax.axis_size("seq")
    m = lax.axis_size("head")
    length, heads, dh = queries.shape
    place = lax.axis_index("seq")
    parity = place % 2
    line = n // 2
    where_on_line = place // 2
    columns = out_weight.shape[1]
    width = columns // n

    docs = doc_ids.astype(F32)
    tail = (docs == docs[-1]).astype(BF)
    own_state = jnp.einsum(
        "shd,she->hde", key_vectors * tail[:, None, None], value_vectors, preferred_element_type=F32
    )
    state_low, before = window(own_state, docs[-1:], 1)

    pieces = grad_out.reshape(length, -1, 2, width)
    for_partner = lax.dynamic_index_in_dim(pieces, 1 - parity, 2, keepdims=False)
    from_partner = swap(for_partner, "seq", 1)
    both = jnp.concatenate([grad_out, from_partner.reshape(length, -1)], axis=1)
    gathered = gather_heads(both)
    share = columns // m
    cotangent = gathered[:, :, :share].reshape(length, columns)
    partner_cot = gathered[:, :, share:].reshape(length, line, width)
    own_cot = lax.dynamic_index_in_dim(
        cotangent.reshape(length, line, 2, width), parity, 2, keepdims=False
    )

    causal = lax.broadcasted_iota(jnp.int32, (length, length), 0) >= lax.broadcasted_iota(
        jnp.int32, (length, length), 1
    )
    pairs = causal & (docs[:, None] == docs[None, :])
    reads = (docs == before[0]).astype(F32)
    scores = jnp.einsum("thd,shd->hts", queries, key_vectors, preferred_element_type=F32)
    scores_low = jnp.where(pairs[None], scores, 0.0).astype(BF)
    attn = jnp.einsum("hts,she->the", scores_low, value_vectors, preferred_element_type=F32)
    attn = attn + reads[:, None, None] * jnp.einsum(
        "thd,hde->the", queries, state_low, preferred_element_type=F32
    )
    scale = lax.rsqrt(jnp.mean(attn * attn, axis=-1, keepdims=True) + 1e-05)
    normed_f = attn * scale
    normed = normed_f.astype(BF).reshape(length, -1)
    partner_normed = swap(normed, "seq", 1)

    grad_normed = lax.dot_general(
        cotangent, out_weight, (((1,), (1,)), ((), ())), preferred_element_type=F32
    ).reshape(attn.shape)
    grad_attn = (
        scale * (grad_normed - normed_f * jnp.mean(grad_normed * normed_f, axis=-1, keepdims=True))
    ).astype(BF)
    head_mask = (docs == docs[0]).astype(BF)
    own_back = jnp.einsum(
        "thd,the->hde", queries * head_mask[:, None, None], grad_attn, preferred_element_type=F32
    )
    back_low, after = window(own_back, docs[:1], -1)
    writes = (docs == after[0]).astype(F32)

    partial_out = jnp.dot(normed, out_weight, preferred_element_type=F32)
    layer_out = scatter_heads(partial_out)

    def share_of(step):
        goal = (where_on_line + step) % line
        mine = lax.dynamic_index_in_dim(own_cot, goal, 1, keepdims=False)
        theirs = lax.dynamic_index_in_dim(partner_cot, goal, 1, keepdims=False)
        over_tokens = (((0,), (0,)), ((), ()))
        return lax.dot_general(
            normed, mine, over_tokens, preferred_element_type=F32
        ) + lax.dot_general(partner_normed, theirs, over_tokens, preferred_element_type=F32)

    arrived = []
    for step in list(range(1, line)):
        route = [
            (2 * a + b, 2 * ((a + step) % line) + b) for a in range(line) for b in range(2)
        ]
        arrived.append(lax.ppermute(share_of(step).astype(BF), "seq", route))
    grad_weight = share_of(0)
    for part in arrived:
        grad_weight = grad_weight + part.astype(F32)

    grad_scores = jnp.einsum("the,she->hts", grad_attn, value_vectors, preferred_element_type=F32)
    grad_scores = jnp.where(pairs[None], grad_scores, 0.0).astype(BF)
    grad_queries = jnp.einsum("hts,shd->thd", grad_scores, key_vectors, preferred_element_type=F32)
    grad_queries = grad_queries + reads[:, None, None] * jnp.einsum(
        "the,hde->thd", grad_attn, state_low, preferred_element_type=F32
    )
    grad_keys = jnp.einsum("hts,thd->shd", grad_scores, queries, preferred_element_type=F32)
    grad_keys = grad_keys + writes[:, None, None] * jnp.einsum(
        "she,hde->shd", value_vectors, back_low, preferred_element_type=F32
    )
    grad_values = jnp.einsum("hts,the->she", scores_low, grad_attn, preferred_element_type=F32)
    grad_values = grad_values + writes[:, None, None] * jnp.einsum(
        "shd,hde->she", key_vectors, back_low, preferred_element_type=F32
    )
    return (
        layer_out,
        grad_queries.astype(BF),
        grad_keys.astype(BF),
        grad_values.astype(BF),
        grad_weight,
    )


def solution(mesh):
    placed = (
        P("seq", "head", None),
        P("seq", "head", None),
        P("seq", "head", None),
        P("seq"),
        P("head", None),
        P("seq", "head"),
    )
    return jax.shard_map(
        shards,
        mesh=mesh,
        in_specs=placed,
        out_specs=(
            P("seq", "head"),
            P("seq", "head", None),
            P("seq", "head", None),
            P("seq", "head", None),
            P("head", "seq"),
        ),
        check_vma=False,
    )
```

```python
import jax
import jax.numpy as jnp
from jax import lax
from jax.sharding import PartitionSpec as P


BF = jnp.bfloat16
F32 = jnp.float32


def shift(block, distance):
    n = lax.axis_size("seq")
    route = [(i, i + distance) for i in range(n) if 0 <= i + distance < n]
    return lax.ppermute(block, "seq", route)


def swap(block, axis, bit):
    n = lax.axis_size(axis)
    return lax.ppermute(block, axis, [(i, i ^ bit) for i in range(n)])


def gather_heads(block, first):
    me = lax.axis_index("head")
    bit = lax.axis_size("head") // 2
    columns = block.shape[1]
    held = [block]
    while bit:
        other = swap(jnp.concatenate(held, axis=1), "head", bit)
        if first is not None:
            other, first = lax.optimization_barrier((other, first))
            first = None
        high = (me // bit) % 2 == 1
        merged = []
        for i, own in enumerate(held):
            theirs = other[:, i * columns : (i + 1) * columns]
            merged += [jnp.where(high, theirs, own), jnp.where(high, own, theirs)]
        held = merged
        bit //= 2
    return held


def scatter_heads(partial):
    me = lax.axis_index("head")
    size = lax.axis_size("head")
    share = partial.shape[1] // size
    held = [partial[:, i * share : (i + 1) * share] for i in range(size)]
    bit = 1
    while bit < size:
        high = (me // bit) % 2 == 1
        couples = list(zip(held[0::2], held[1::2]))
        given = jnp.concatenate([jnp.where(high, a, b).astype(BF) for a, b in couples], axis=1)
        other = swap(given, "head", bit)
        held = [
            jnp.where(high, b, a) + other[:, i * share : (i + 1) * share].astype(F32)
            for i, (a, b) in enumerate(couples)
        ]
        bit *= 2
    return held[0].astype(BF)


def with_doc(state, doc):
    rows = jnp.broadcast_to(doc.astype(BF)[:, None], (16, state.shape[-1]))
    return jnp.concatenate([state.astype(BF).reshape(-1, state.shape[-1]), rows], axis=0)


def window(total, sign, first=None):
    rows = lax.broadcasted_iota(jnp.int32, (total.shape[0], 1), 0) < total.shape[0] - 16
    span = 1
    while span < lax.axis_size("seq") // 2:
        far = shift(total, sign * span)
        if first is not None and 4 * span >= lax.axis_size("seq"):
            far, first = lax.optimization_barrier((far, first))
        same = (far[-16:-15] == total[-16:-15]) & rows
        total = total + jnp.where(same, far, jnp.zeros_like(far))
        span *= 2
    return total


def shards(queries, key_vectors, value_vectors, doc_ids, out_weight, grad_out):
    n = lax.axis_size("seq")
    m = lax.axis_size("head")
    length, heads, dh = queries.shape
    place = lax.axis_index("seq")
    parity = place % 2
    line = n // 2
    where_on_line = place // 2
    columns = out_weight.shape[1]
    width = columns // n

    docs = doc_ids.astype(F32)
    tail = (docs == docs[-1]).astype(BF)
    own_state = jnp.einsum(
        "shd,she->hde", key_vectors * tail[:, None, None], value_vectors, preferred_element_type=F32
    )
    near_flat = shift(with_doc(own_state, docs[-1:]), 1)
    own_gathered = gather_heads(grad_out, near_flat)
    near_flat, grad_out = lax.optimization_barrier((near_flat, grad_out))
    flat = window(near_flat, 1)
    before = flat[-16, :1].astype(F32)
    state_low = flat[:-16].reshape(own_state.shape)

    causal = lax.broadcasted_iota(jnp.int32, (length, length), 0) >= lax.broadcasted_iota(
        jnp.int32, (length, length), 1
    )
    pairs = causal & (docs[:, None] == docs[None, :])
    reads = (docs == before[0]).astype(F32)
    scores = jnp.einsum("thd,shd->hts", queries, key_vectors, preferred_element_type=F32)
    scores_low = jnp.where(pairs[None], scores, 0.0).astype(BF)
    attn = jnp.einsum("hts,she->the", scores_low, value_vectors, preferred_element_type=F32)
    attn = attn + reads[:, None, None] * jnp.einsum(
        "thd,hde->the", queries, state_low, preferred_element_type=F32
    )
    scale = lax.rsqrt(jnp.mean(attn * attn, axis=-1, keepdims=True) + 1e-05)
    normed_f = attn * scale
    normed = normed_f.astype(BF).reshape(length, -1)
    partner_normed = swap(normed, "seq", 1)

    share = columns // m
    odd = parity == 1
    for_partner = [
        jnp.where(odd, grad_out[:, i : i + width], grad_out[:, i + width : i + 2 * width])
        for i in range(0, share, 2 * width)
    ]
    from_partner = swap(jnp.concatenate(for_partner, axis=1), "seq", 1)
    cotangent = jnp.concatenate(own_gathered, axis=1)
    partner_cot = jnp.concatenate(gather_heads(from_partner, normed), axis=1)

    grad_normed = lax.dot_general(
        cotangent, out_weight, (((1,), (1,)), ((), ())), preferred_element_type=F32
    ).reshape(attn.shape)
    grad_attn = (
        scale * (grad_normed - normed_f * jnp.mean(grad_normed * normed_f, axis=-1, keepdims=True))
    ).astype(BF)
    head_mask = (docs == docs[0]).astype(BF)
    own_back = jnp.einsum(
        "thd,the->hde", queries * head_mask[:, None, None], grad_attn, preferred_element_type=F32
    )
    near_flat = shift(with_doc(own_back, docs[:1]), -1)

    def share_of(step):
        goal = (where_on_line + step) % line
        mine = lax.dynamic_slice_in_dim(cotangent, (2 * goal + parity) * width, width, 1)
        theirs = lax.dynamic_slice_in_dim(partner_cot, goal * width, width, 1)
        over_tokens = (((0,), (0,)), ((), ()))
        return lax.dot_general(
            normed, mine, over_tokens, preferred_element_type=F32
        ) + lax.dot_general(partner_normed, theirs, over_tokens, preferred_element_type=F32)

    terms = [share_of(step).astype(BF) for step in range(1, line)]
    terms, near_flat = lax.optimization_barrier((terms, near_flat))
    terms, grad_attn_in, normed_out = lax.optimization_barrier((terms, grad_attn, normed))
    partial_out = jnp.dot(normed_out, out_weight, preferred_element_type=F32)
    layer_out = scatter_heads(partial_out)
    flat = window(near_flat, -1, layer_out)
    after = flat[-16, :1].astype(F32)
    back_low = flat[:-16].reshape(own_back.shape)
    writes = (docs == after[0]).astype(F32)
    arrived = []
    for step, term in enumerate(terms, 1):
        route = [
            (2 * a + b, 2 * ((a + step) % line) + b) for a in range(line) for b in range(2)
        ]
        arrived.append(lax.ppermute(term, "seq", route))
    own_term = share_of(0)

    grad_scores = jnp.einsum("the,she->hts", grad_attn_in, value_vectors, preferred_element_type=F32)
    grad_scores = jnp.where(pairs[None], grad_scores, 0.0).astype(BF)
    grad_queries = jnp.einsum("hts,shd->thd", grad_scores, key_vectors, preferred_element_type=F32)
    grad_queries = grad_queries + reads[:, None, None] * jnp.einsum(
        "the,hde->thd", grad_attn_in, state_low, preferred_element_type=F32
    )
    grad_keys = jnp.einsum("hts,thd->shd", grad_scores, queries, preferred_element_type=F32)
    grad_keys = grad_keys + writes[:, None, None] * jnp.einsum(
        "she,hde->shd", value_vectors, back_low, preferred_element_type=F32
    )
    grad_values = jnp.einsum("hts,the->she", scores_low, grad_attn_in, preferred_element_type=F32)
    grad_values = grad_values + writes[:, None, None] * jnp.einsum(
        "shd,hde->she", key_vectors, back_low, preferred_element_type=F32
    )
    arrived, layer_out = lax.optimization_barrier((arrived, layer_out))
    grad_weight = own_term
    for part in arrived:
        grad_weight = grad_weight + part.astype(F32)
    return (
        layer_out,
        grad_queries.astype(BF),
        grad_keys.astype(BF),
        grad_values.astype(BF),
        grad_weight,
    )


def solution(mesh):
    placed = (
        P("seq", "head", None),
        P("seq", "head", None),
        P("seq", "head", None),
        P("seq"),
        P("head", None),
        P("seq", "head"),
    )
    return jax.shard_map(
        shards,
        mesh=mesh,
        in_specs=placed,
        out_specs=(
            P("seq", "head"),
            P("seq", "head", None),
            P("seq", "head", None),
            P("seq", "head", None),
            P("head", "seq"),
        ),
        check_vma=False,
    )
```

```python
import jax
import jax.numpy as jnp
from jax import lax
from jax.sharding import PartitionSpec as P


BF = jnp.bfloat16
F32 = jnp.float32


def shift(block, distance):
    n = lax.axis_size("seq")
    route = [(i, i + distance) for i in range(n) if 0 <= i + distance < n]
    return lax.ppermute(block, "seq", route)


def swap(block, axis, bit):
    n = lax.axis_size(axis)
    return lax.ppermute(block, axis, [(i, i ^ bit) for i in range(n)])


def gather_heads(block, first):
    me = lax.axis_index("head")
    bit = lax.axis_size("head") // 2
    columns = block.shape[1]
    held = [block]
    while bit:
        other = swap(jnp.concatenate(held, axis=1), "head", bit)
        if first is not None:
            other, first = lax.optimization_barrier((other, first))
            first = None
        high = (me // bit) % 2 == 1
        merged = []
        for i, own in enumerate(held):
            theirs = other[:, i * columns : (i + 1) * columns]
            merged += [jnp.where(high, theirs, own), jnp.where(high, own, theirs)]
        held = merged
        bit //= 2
    return held


def scatter_heads(partial):
    me = lax.axis_index("head")
    size = lax.axis_size("head")
    share = partial.shape[1] // size
    held = [partial[:, i * share : (i + 1) * share] for i in range(size)]
    bit = 1
    while bit < size:
        high = (me // bit) % 2 == 1
        couples = list(zip(held[0::2], held[1::2]))
        given = jnp.concatenate([jnp.where(high, a, b).astype(BF) for a, b in couples], axis=1)
        other = swap(given, "head", bit)
        held = [
            jnp.where(high, b, a) + other[:, i * share : (i + 1) * share].astype(F32)
            for i, (a, b) in enumerate(couples)
        ]
        bit *= 2
    return held[0].astype(BF)


def with_doc(state, doc):
    rows = jnp.broadcast_to(doc.astype(BF)[:, None], (16, state.shape[-1]))
    return jnp.concatenate([state.astype(BF).reshape(-1, state.shape[-1]), rows], axis=0)


def window(total, sign, first=None, span=1, stop=None):
    rows = lax.broadcasted_iota(jnp.int32, (total.shape[0], 1), 0) < total.shape[0] - 16
    while span < (stop or lax.axis_size("seq") // 2):
        far = shift(total, sign * span)
        if first is not None and 4 * span >= lax.axis_size("seq"):
            far, first = lax.optimization_barrier((far, first))
        same = (far[-16:-15] == total[-16:-15]) & rows
        total = total + jnp.where(same, far, jnp.zeros_like(far))
        span *= 2
    return total


def shards(queries, key_vectors, value_vectors, doc_ids, out_weight, grad_out):
    n = lax.axis_size("seq")
    m = lax.axis_size("head")
    length, heads, dh = queries.shape
    place = lax.axis_index("seq")
    parity = place % 2
    line = n // 2
    where_on_line = place // 2
    columns = out_weight.shape[1]
    width = columns // n

    docs = doc_ids.astype(F32)
    tail = (docs == docs[-1]).astype(BF)
    own_state = jnp.einsum(
        "shd,she->hde", key_vectors * tail[:, None, None], value_vectors, preferred_element_type=F32
    )
    near_flat = shift(with_doc(own_state, docs[-1:]), 1)
    own_gathered = gather_heads(grad_out, near_flat)
    near_flat, grad_out = lax.optimization_barrier((near_flat, grad_out))
    flat = window(near_flat, 1)
    before = flat[-16, :1].astype(F32)
    state_low = flat[:-16].reshape(own_state.shape)

    causal = lax.broadcasted_iota(jnp.int32, (length, length), 0) >= lax.broadcasted_iota(
        jnp.int32, (length, length), 1
    )
    pairs = causal & (docs[:, None] == docs[None, :])
    reads = (docs == before[0]).astype(F32)
    scores = jnp.einsum("thd,shd->hts", queries, key_vectors, preferred_element_type=F32)
    scores_low = jnp.where(pairs[None], scores, 0.0).astype(BF)
    attn = jnp.einsum("hts,she->the", scores_low, value_vectors, preferred_element_type=F32)
    attn = attn + reads[:, None, None] * jnp.einsum(
        "thd,hde->the", queries, state_low, preferred_element_type=F32
    )
    scale = lax.rsqrt(jnp.mean(attn * attn, axis=-1, keepdims=True) + 1e-05)
    normed_f = attn * scale
    normed = normed_f.astype(BF).reshape(length, -1)
    partner_normed = swap(normed, "seq", 1)

    share = columns // m
    odd = parity == 1
    for_partner = [
        jnp.where(odd, grad_out[:, i : i + width], grad_out[:, i + width : i + 2 * width])
        for i in range(0, share, 2 * width)
    ]
    from_partner = swap(jnp.concatenate(for_partner, axis=1), "seq", 1)
    cotangent = jnp.concatenate(own_gathered, axis=1)
    partner_cot = jnp.concatenate(gather_heads(from_partner, normed), axis=1)

    grad_normed = lax.dot_general(
        cotangent, out_weight, (((1,), (1,)), ((), ())), preferred_element_type=F32
    ).reshape(attn.shape)
    grad_attn = (
        scale * (grad_normed - normed_f * jnp.mean(grad_normed * normed_f, axis=-1, keepdims=True))
    ).astype(BF)
    head_mask = (docs == docs[0]).astype(BF)
    own_back = jnp.einsum(
        "thd,the->hde", queries * head_mask[:, None, None], grad_attn, preferred_element_type=F32
    )
    near_flat = shift(with_doc(own_back, docs[:1]), -1)

    def share_of(step):
        goal = (where_on_line + step) % line
        mine = lax.dynamic_slice_in_dim(cotangent, (2 * goal + parity) * width, width, 1)
        theirs = lax.dynamic_slice_in_dim(partner_cot, goal * width, width, 1)
        over_tokens = (((0,), (0,)), ((), ()))
        return lax.dot_general(
            normed, mine, over_tokens, preferred_element_type=F32
        ) + lax.dot_general(partner_normed, theirs, over_tokens, preferred_element_type=F32)

    terms = [share_of(step).astype(BF) for step in range(1, line)]
    mid_flat = window(near_flat, -1, stop=n // 4)
    terms, mid_flat = lax.optimization_barrier((terms, mid_flat))
    terms, grad_attn_in, normed_out = lax.optimization_barrier((terms, grad_attn, normed))
    partial_out = jnp.dot(normed_out, out_weight, preferred_element_type=F32)
    layer_out = scatter_heads(partial_out)
    flat = window(mid_flat, -1, layer_out, n // 4)
    after = flat[-16, :1].astype(F32)
    back_low = flat[:-16].reshape(own_back.shape)
    writes = (docs == after[0]).astype(F32)
    arrived = []
    for step, term in enumerate(terms, 1):
        route = [
            (2 * a + b, 2 * ((a + step) % line) + b) for a in range(line) for b in range(2)
        ]
        arrived.append(lax.ppermute(term, "seq", route))
    own_term = share_of(0)

    grad_scores = jnp.einsum("the,she->hts", grad_attn_in, value_vectors, preferred_element_type=F32)
    grad_scores = jnp.where(pairs[None], grad_scores, 0.0).astype(BF)
    grad_queries = jnp.einsum("hts,shd->thd", grad_scores, key_vectors, preferred_element_type=F32)
    grad_queries = grad_queries + reads[:, None, None] * jnp.einsum(
        "the,hde->thd", grad_attn_in, state_low, preferred_element_type=F32
    )
    grad_keys = jnp.einsum("hts,thd->shd", grad_scores, queries, preferred_element_type=F32)
    grad_keys = grad_keys + writes[:, None, None] * jnp.einsum(
        "she,hde->shd", value_vectors, back_low, preferred_element_type=F32
    )
    grad_values = jnp.einsum("hts,the->she", scores_low, grad_attn_in, preferred_element_type=F32)
    grad_values = grad_values + writes[:, None, None] * jnp.einsum(
        "shd,hde->she", key_vectors, back_low, preferred_element_type=F32
    )
    arrived, layer_out = lax.optimization_barrier((arrived, layer_out))
    grad_weight = own_term
    for part in arrived:
        grad_weight = grad_weight + part.astype(F32)
    return (
        layer_out,
        grad_queries.astype(BF),
        grad_keys.astype(BF),
        grad_values.astype(BF),
        grad_weight,
    )


def solution(mesh):
    placed = (
        P("seq", "head", None),
        P("seq", "head", None),
        P("seq", "head", None),
        P("seq"),
        P("head", None),
        P("seq", "head"),
    )
    return jax.shard_map(
        shards,
        mesh=mesh,
        in_specs=placed,
        out_specs=(
            P("seq", "head"),
            P("seq", "head", None),
            P("seq", "head", None),
            P("seq", "head", None),
            P("head", "seq"),
        ),
        check_vma=False,
    )
```
